32 devices in a mesh: groups: 2 (over x), ctx: 16 (over z, y, core).
Axes of the slice: x: 2, y: 2, z: 4, core: 2. Of those that a mesh axis runs over, the one named last changes fastest.
Arguments:
- queries: bfloat16 [8192, 512], P(('groups', 'ctx')), parts along dimension 0, may hold values from -6 to 6
- keys: bfloat16 [8192, 512], P(('groups', 'ctx')), parts along dimension 0, may hold values from -6 to 6
- values: bfloat16 [8192, 512], P(('groups', 'ctx')), parts along dimension 0, may hold values from -6 to 6
- grad_out: bfloat16 [8192, 512], P(('groups', 'ctx')), parts along dimension 0, may hold values from -6 to 6
- far_blocks: int32 [64, 3], P(('groups', 'ctx')), parts along dimension 0, may hold values from 0 to 31, as said below
- far_levels: int32 [32], P(('groups', 'ctx')), parts along dimension 0, may hold values from 0 to 3
Outputs:
- attended: bfloat16 [8192, 512], P(('groups', 'ctx')), parts along dimension 0
- grad_queries: bfloat16 [8192, 512], P(('groups', 'ctx')), parts along dimension 0
- grad_keys: bfloat16 [8192, 512], P(('groups', 'ctx')), parts along dimension 0
- grad_values: bfloat16 [8192, 512], P(('groups', 'ctx')), parts along dimension 0
The draws below stay inside these ranges and needn't reach their ends.
There are 2 independent parts, one for each index of `groups`. The reference program is written for one: setup_inputs(seed, part) draws one part's arguments, and reference() takes and returns one part's arrays. A program takes and returns all parts, laid end to end along the dimension named above; each array names one. Nothing has to cross between parts.
Inputs may be any that keep to these rules, and one draw needn't show every extreme that they name: far_blocks[b, l] names a block of the shard whose index differs from b // 2 by exclusive or with 16 // 2**(l + 1).
All inputs are finite; a program needn't handle non-finite values.
Results may differ from the reference program's by a relative error of at most 0.012.
Values may be sent and summed in bfloat16 or wider, within the bound.
No kernel may reach another device: no remote copies, remote signals or barrier semaphores. Data moves between devices by JAX's collectives and lax.ppermute only.
A program may use at most 64 MiB of HBM per device.

```python
import jax
import jax.numpy as jnp
from jax import lax

HEADS = 8
HEAD_DIM = 64
WIDTH = 512
BLOCK = 128
REACH = 2
LEVELS = 3
BLK_DEV = 2
NB = 32
TOKENS = 4096
N_CTX = 16


def float_basis(key, salt):
    return jax.random.truncated_normal(jax.random.fold_in(key, salt), -4.0, 4.0, (TOKENS, WIDTH), jnp.float32)


def draw_queries(key, part):
    filled = float_basis(key, 1)
    return filled.astype(jnp.bfloat16)


def draw_keys(key, part):
    filled = float_basis(key, 2)
    return filled.astype(jnp.bfloat16)


def draw_far_blocks(key, part):
    devices = NB // BLK_DEV
    block_ids = jnp.arange(NB, dtype=jnp.int32)[:, None]
    level_ids = jnp.arange(LEVELS, dtype=jnp.int32)[None, :]
    owner_dev = block_ids // BLK_DEV
    partner = jnp.bitwise_xor(owner_dev, jnp.right_shift(jnp.int32(devices), level_ids + 1))
    local_pick = jax.random.randint(jax.random.fold_in(key, 11), (NB, LEVELS), 0, BLK_DEV, dtype=jnp.int32)
    top_block = devices // 2 * BLK_DEV - 1
    low_block = devices // 2 * BLK_DEV
    local_pick = jnp.where((block_ids == top_block) & (level_ids == 0), BLK_DEV - 1, local_pick)
    local_pick = jnp.where((block_ids == low_block) & (level_ids == 0), 0, local_pick)
    return (partner * BLK_DEV + local_pick).astype(jnp.int32)


def draw_far_levels(key, part):
    devices = NB // BLK_DEV
    counts = jax.random.randint(jax.random.fold_in(key, 21), (devices,), 0, LEVELS + 1, dtype=jnp.int32)
    shuffled = jax.random.permutation(jax.random.fold_in(key, 22), devices)
    counts = counts.at[shuffled[0]].set(LEVELS)
    counts = counts.at[shuffled[1]].set(0)
    return counts


def shard_levels(key, dims, cuts, smallest, largest):
    gain, own = 1.0, jax.random.fold_in(key, 6)
    for dim, blocks in cuts:
        draws = jnp.exp(jax.random.uniform(jax.random.fold_in(own, dim), (blocks,), jnp.float32, smallest / len(cuts), largest / len(cuts)))
        gain = gain * jnp.repeat(draws, dims[dim] // blocks).reshape([-1 if axis == dim else 1 for axis in range(len(dims))])
    return gain


def scatter_about(rng, shape, width, bound, pieces=(), kind=jnp.bfloat16):
    gain = shard_levels(rng, shape, pieces, -0.22, 0.18) if pieces else 1.0
    entries = jax.random.normal(rng, shape, jnp.float32) * width * gain
    return jnp.minimum(jnp.maximum(entries, -bound), bound).astype(kind)


def setup_inputs(seed: int = 0, part: int = 0) -> dict:
    key_of = jax.random.split(jax.random.key(seed), 7)
    own_keys = jax.random.split(jax.random.fold_in(key_of[6], part), 7)
    queries = draw_queries(jax.random.fold_in(jax.random.fold_in(key_of[6], part), 71), part)
    keys = draw_keys(jax.random.fold_in(jax.random.fold_in(key_of[6], part), 71), part)
    values = scatter_about(own_keys[2], (TOKENS, WIDTH), 1.0, 6.0, ((0, 16),))
    grad_out = scatter_about(own_keys[3], (TOKENS, WIDTH), 1.0, 6.0, ((0, 16),))
    far_blocks = draw_far_blocks(jax.random.fold_in(jax.random.fold_in(key_of[6], part), 71), part)
    far_levels = draw_far_levels(jax.random.fold_in(jax.random.fold_in(key_of[6], part), 71), part)
    return dict(queries=queries, keys=keys, values=values, grad_out=grad_out, far_blocks=far_blocks, far_levels=far_levels)


def reference(queries, keys, values, grad_out, far_blocks, far_levels):
    total_blocks = BLK_DEV * N_CTX
    score_scale = HEAD_DIM ** -0.5
    head_shape = (total_blocks, BLOCK, HEADS, HEAD_DIM)
    query_all = queries.reshape(head_shape)
    key_all = keys.reshape(head_shape)
    value_all = values.reshape(head_shape)
    grad_all = grad_out.reshape(head_shape)
    offsets = jnp.arange(-REACH, REACH + 1, dtype=jnp.int32)
    levels = jnp.arange(LEVELS, dtype=jnp.int32)

    def step(accums, block_id):
        key_acc, value_acc = accums
        near_ids = block_id + offsets
        near_valid = (near_ids >= 0) & (near_ids < total_blocks)
        near_ids = jnp.clip(near_ids, 0, total_blocks - 1)
        far_ids = far_blocks[block_id]
        far_valid = levels < far_levels[block_id // BLK_DEV]
        key_ids = jnp.concatenate([near_ids, far_ids]).astype(jnp.int32)
        valid = jnp.repeat(jnp.concatenate([near_valid, far_valid]), BLOCK)
        key_part = key_all[key_ids].reshape(-1, HEADS, HEAD_DIM).astype(jnp.float32)
        value_part = value_all[key_ids].reshape(-1, HEADS, HEAD_DIM).astype(jnp.float32)
        query_rows = query_all[block_id].astype(jnp.float32)
        cotangent = grad_all[block_id].astype(jnp.float32)
        scores = jnp.einsum('qhd,khd->hqk', query_rows, key_part) * score_scale
        scores = jnp.where(valid[None, None, :], scores, -1e30)
        peak = jnp.max(scores, axis=-1, keepdims=True)
        log_total = peak + jnp.log(jnp.sum(jnp.exp(scores - peak), axis=-1, keepdims=True))
        weights = jnp.exp(scores - log_total)
        weights_low = weights.astype(jnp.bfloat16)
        mixed = jnp.einsum('hqk,khd->qhd', weights_low.astype(jnp.float32), value_part).astype(jnp.bfloat16)
        row_delta = jnp.einsum('qhd,qhd->hq', cotangent, mixed.astype(jnp.float32))
        grad_weights = jnp.einsum('qhd,khd->hqk', cotangent, value_part)
        grad_scores = (weights * (grad_weights - row_delta[..., None])).astype(jnp.bfloat16)
        grad_scores32 = grad_scores.astype(jnp.float32)
        grad_query = (jnp.einsum('hqk,khd->qhd', grad_scores32, key_part) * score_scale).astype(jnp.bfloat16)
        grad_key = jnp.einsum('hqk,qhd->khd', grad_scores32, query_rows) * score_scale
        grad_value = jnp.einsum('hqk,qhd->khd', weights_low.astype(jnp.float32), cotangent)
        count = key_ids.shape[0]
        key_acc = key_acc.at[key_ids].add(grad_key.reshape(count, BLOCK, HEADS * HEAD_DIM))
        value_acc = value_acc.at[key_ids].add(grad_value.reshape(count, BLOCK, HEADS * HEAD_DIM))
        return (key_acc, value_acc), (mixed, grad_query)

    zeros_init = jnp.zeros((total_blocks, BLOCK, HEADS * HEAD_DIM), jnp.float32)
    (key_acc, value_acc), (mixed, grad_query) = lax.scan(step, (zeros_init, zeros_init), jnp.arange(total_blocks, dtype=jnp.int32))
    flat = (total_blocks * BLOCK, HEADS * HEAD_DIM)
    return (mixed.reshape(flat), grad_query.reshape(flat), key_acc.astype(jnp.bfloat16).reshape(flat), value_acc.astype(jnp.bfloat16).reshape(flat))
```

```python
import functools

import jax
import jax.numpy as jnp
from jax import lax
from jax.experimental import pallas as pl
from jax.experimental.pallas import tpu as pltpu
from jax.sharding import PartitionSpec as P

HEADS = 8
HEAD_DIM = 64
WIDTH = 512
BLOCK = 128
REACH = 2
LEVELS = 3
BLK_DEV = 2
ROWS = BLK_DEV * BLOCK
PAIR = 2 * HEAD_DIM
PAIRS = WIDTH // PAIR
SCALE = HEAD_DIM ** (-0.5)
MASKED = -1e30


NT = (((1,), (1,)), ((), ()))
NN = (((1,), (0,)), ((), ()))


def dot(a, b, dims):
    return lax.dot_general(a, b, dims, preferred_element_type=jnp.float32)


def left_half(shape):
    return lax.broadcasted_iota(jnp.int32, shape, 1) < HEAD_DIM


def two_heads(tile):
    low = left_half(tile.shape)
    zero = jnp.zeros_like(tile)
    return jnp.concatenate([jnp.where(low, tile, zero), jnp.where(low, zero, tile)], axis=0)


def one_tile(stacked):
    return jnp.where(left_half((BLOCK, PAIR)), stacked[:BLOCK], stacked[BLOCK:])


def query_kernel(
    picks_ref,
    bias_ref,
    q_ref,
    do_ref,
    *refs,
):
    key_refs = refs[0 : 2 * (3 + LEVELS) : 2]
    value_refs = refs[1 : 2 * (3 + LEVELS) : 2]
    out_ref, grad_ref, near_ref, far_ref = refs[2 * (3 + LEVELS) :]

    def gathered(sources, block):
        parts = []
        for offset in range(2 * REACH + 1):
            at = block + offset
            source, row = divmod(at, BLK_DEV)
            parts.append(sources[source][row * BLOCK : (row + 1) * BLOCK, :])
        for level in range(LEVELS):
            start = pl.multiple_of(picks_ref[block * LEVELS + level] * BLOCK, BLOCK)
            parts.append(sources[3 + level][pl.ds(start, BLOCK), :])
        return jnp.concatenate(parts, axis=0)

    near_rows = []
    delta_rows = []
    for block in range(BLK_DEV):
        rows = slice(block * BLOCK, (block + 1) * BLOCK)
        query = two_heads((q_ref[rows, :].astype(jnp.float32) * SCALE).astype(jnp.bfloat16))
        cotangent = two_heads(do_ref[rows, :])
        key = gathered(key_refs, block)
        value = gathered(value_refs, block)
        scores = dot(query, key, NT)
        pieces = []
        for j in range(2 * REACH + 1 + LEVELS):
            piece = scores[:, j * BLOCK : (j + 1) * BLOCK]
            if j < 2 * REACH + 1:
                source = (block + j) // BLK_DEV
                if source != 1:
                    piece = piece + bias_ref[source // 2]
            else:
                piece = piece + bias_ref[2 + j - 2 * REACH - 1]
            pieces.append(piece)
        scores = jnp.concatenate(pieces, axis=1)
        peak = jnp.max(scores, axis=1, keepdims=True)
        weights = jnp.exp(scores - peak)
        total = jnp.sum(weights, axis=1, keepdims=True)
        weights = weights * (1.0 / total)
        low = weights.astype(jnp.bfloat16)
        mixed = one_tile(dot(low, value, NN)).astype(jnp.bfloat16)
        out_ref[rows, :] = mixed
        mixed = mixed.astype(jnp.float32)
        delta = jnp.sum(
            cotangent.astype(jnp.float32) * jnp.concatenate([mixed, mixed], axis=0), axis=1, keepdims=True
        )
        grad_weights = dot(cotangent, value, NT)
        grad_scores = (weights * (grad_weights - delta)).astype(jnp.bfloat16)
        grad_query = one_tile(dot(grad_scores, key, NN)) * SCALE
        grad_ref[rows, :] = grad_query.astype(jnp.bfloat16)
        lane = lax.broadcasted_iota(jnp.int32, (2 * BLOCK, BLOCK), 1)
        log_total = peak + jnp.log(total)
        turned = jnp.where(lane == 0, log_total, delta).T
        near_rows.append(turned[0:1, :])
        delta_rows.append(turned[1:2, :])
    pad = jnp.zeros((1, 2 * BLOCK), jnp.float32)
    near_ref[0] = jnp.concatenate(near_rows + delta_rows + [pad] * 4, axis=0)
    for level in range(LEVELS):
        seen = []
        for target in range(BLK_DEV):
            for block in range(BLK_DEV):
                hit = jnp.logical_and(
                    picks_ref[block * LEVELS + level] == target, bias_ref[2 + level] == 0.0
                )
                seen.append(jnp.where(hit, near_rows[block], -MASKED))
        far_ref[level, 0] = jnp.concatenate(seen + delta_rows + [pad] * 2, axis=0)


def pair_terms(key, value, tile_q, tile_do, log_total, delta):
    query = two_heads((tile_q.astype(jnp.float32) * SCALE).astype(jnp.bfloat16))
    cotangent = two_heads(tile_do)
    weights = jnp.exp(dot(key, query, NT) - log_total)
    grad_weights = dot(value, cotangent, NT)
    grad_scores = (weights * (grad_weights - delta)).astype(jnp.bfloat16)
    grad_key = dot(grad_scores, query, NN)
    grad_value = dot(weights.astype(jnp.bfloat16), cotangent, NN)
    return grad_key, grad_value


def key_kernel(kinds, carried, final, *refs):
    key_ref, value_ref = refs[0:2]
    at = 2
    if carried:
        key_sum = refs[at][...]
        value_sum = refs[at + 1][...]
        at += 2
    else:
        key_sum = jnp.zeros((ROWS, PAIR), jnp.float32)
        value_sum = jnp.zeros((ROWS, PAIR), jnp.float32)
    key = key_ref[...]
    value = value_ref[...]
    for kind in kinds:
        q_ref, do_ref, stat_ref = refs[at : at + 3]
        at += 3
        for block in range(BLK_DEV):
            rows = slice(block * BLOCK, (block + 1) * BLOCK)
            first, last = (0, BLK_DEV)
            if kind == "left" and block == 0:
                last = 1
            if kind == "right" and block == 1:
                first = 1
            span = slice(first * BLOCK, last * BLOCK)
            if kind == "far":
                log_total = jnp.concatenate(
                    [
                        jnp.broadcast_to(
                            stat_ref[0, target * BLK_DEV + block : target * BLK_DEV + block + 1, :],
                            (BLOCK, 2 * BLOCK),
                        )
                        for target in range(BLK_DEV)
                    ],
                    axis=0,
                )
                delta = stat_ref[0, 4 + block : 5 + block, :]
            else:
                log_total = stat_ref[0, block : block + 1, :]
                delta = stat_ref[0, 2 + block : 3 + block, :]
            grad_key, grad_value = pair_terms(
                key[span], value[span], q_ref[rows, :], do_ref[rows, :], log_total, delta
            )
            empty = jnp.zeros((BLOCK, PAIR), jnp.float32)
            if first == 1:
                grad_key = jnp.concatenate([empty, grad_key], axis=0)
                grad_value = jnp.concatenate([empty, grad_value], axis=0)
            if last == 1:
                grad_key = jnp.concatenate([grad_key, empty], axis=0)
                grad_value = jnp.concatenate([grad_value, empty], axis=0)
            key_sum = key_sum + grad_key
            value_sum = value_sum + grad_value
    gk_ref, gv_ref = refs[at:]
    gk_ref[...] = key_sum.astype(gk_ref.dtype)
    gv_ref[...] = value_sum.astype(gv_ref.dtype)


def first_half(rows=ROWS):
    return pl.BlockSpec((rows, PAIR), lambda p, *_: (0, p))


def second_half(rows=ROWS):
    return pl.BlockSpec((rows, PAIR), lambda p, *_: (0, p + PAIRS))


def run_queries(picks, bias, queries, grad_out, keys, values, received):
    specs = [first_half(), first_half()]
    operands = [queries, grad_out]
    left, right, far = received
    for index, source in enumerate([left, (keys, values), right] + far):
        if index == 1:
            operands += [keys, values]
            specs += [first_half(), first_half()]
        else:
            operands += [source, source]
            specs += [first_half(), second_half()]
    near = jax.ShapeDtypeStruct((PAIRS, 8, 2 * BLOCK), jnp.float32)
    distant = jax.ShapeDtypeStruct((LEVELS, PAIRS, 8, 2 * BLOCK), jnp.float32)
    whole = jax.ShapeDtypeStruct((ROWS, WIDTH), jnp.bfloat16)
    return pl.pallas_call(
        query_kernel,
        out_shape=(whole, whole, near, distant),
        grid_spec=pltpu.PrefetchScalarGridSpec(
            num_scalar_prefetch=2,
            grid=(PAIRS,),
            in_specs=specs,
            out_specs=(
                first_half(),
                first_half(),
                pl.BlockSpec((1, 8, 2 * BLOCK), lambda p, *_: (p, 0, 0)),
                pl.BlockSpec((LEVELS, 1, 8, 2 * BLOCK), lambda p, *_: (0, p, 0, 0)),
            ),
        ),
        cost_estimate=pl.CostEstimate(
            flops=4 * 10**9, bytes_accessed=8 * 2**20, transcendentals=2 * 10**6
        ),
        name="query_side",
    )(picks, bias, *operands)


def run_keys(keys, values, sources, carried=None, final=False):
    specs = [first_half(), first_half()]
    operands = [keys, values]
    if carried is not None:
        operands += list(carried)
        specs += [first_half(), first_half()]
    kinds = []
    for kind, rows, stats in sources:
        kinds.append(kind)
        if kind == "own":
            operands += list(rows)
            specs += [first_half(), first_half()]
        else:
            operands += [rows, rows]
            specs += [first_half(), second_half()]
        operands.append(stats)
        specs.append(pl.BlockSpec((1, 8, 2 * BLOCK), lambda p, *_: (p, 0, 0)))
    kind_out = jax.ShapeDtypeStruct((ROWS, WIDTH), jnp.bfloat16 if final else jnp.float32)
    return pl.pallas_call(
        functools.partial(key_kernel, tuple(kinds), carried is not None, final),
        out_shape=(kind_out, kind_out),
        grid=(PAIRS,),
        in_specs=specs,
        out_specs=(first_half(), first_half()),
        cost_estimate=pl.CostEstimate(
            flops=10**9 * len(kinds), bytes_accessed=len(kinds) * 2**20, transcendentals=10**6
        ),
        name="key_side_" + "_".join(kinds),
    )(*operands)


def on_device(queries, keys, values, grad_out, far_blocks, far_levels):
    size = lax.axis_size("ctx")
    index = lax.axis_index("ctx")
    top_bit = size.bit_length() - 2

    def exchanged(array, level):
        return lax.ppermute(array, "ctx", [(i, i ^ 1 << (top_bit - level)) for i in range(size)])

    def moved(array, by):
        pairs = [(i, i + by) for i in range(size) if 0 <= i + by < size]
        return lax.ppermute(array, "ctx", pairs)

    key_value = jnp.concatenate([keys, values], axis=1)
    kv_far = [None] * LEVELS
    for level in (1, 0):
        kv_far[level] = exchanged(key_value, level)
    kv_left = moved(key_value, 1)
    kv_right = moved(key_value, -1)
    kv_far[2] = exchanged(key_value, 2)

    row_sets = jnp.concatenate([queries, grad_out], axis=1)
    q_far = [None] * LEVELS
    for level in (1, 0):
        q_far[level] = exchanged(row_sets, level)
    q_left = moved(row_sets, 1)
    q_right = moved(row_sets, -1)
    q_far[2] = exchanged(row_sets, 2)

    picks = (far_blocks % BLK_DEV).reshape(-1)
    used = jnp.arange(LEVELS, dtype=jnp.int32) < far_levels[0]
    edges = jnp.stack([index > 0, index < size - 1])
    bias = jnp.where(jnp.concatenate([edges, used]), 0.0, MASKED).astype(jnp.float32)

    attended, grad_queries, near, distant = run_queries(
        picks, bias, queries, grad_out, keys, values, (kv_left, kv_right, kv_far)
    )
    s_far = [exchanged(distant[level], level) for level in range(LEVELS)]
    s_left = moved(near, 1)
    s_right = moved(near, -1)
    carried = run_keys(keys, values, [("own", (queries, grad_out), near)])
    carried = run_keys(
        keys,
        values,
        [
            ("far", q_far[1], s_far[1]),
            ("far", q_far[0], s_far[0]),
            ("left", q_left, s_left),
            ("right", q_right, s_right),
            ("far", q_far[2], s_far[2]),
        ],
        carried,
        True,
    )
    return (attended, grad_queries, *carried)


def solution(mesh):
    rows = P(("groups", "ctx"), None)
    in_specs = (rows, rows, rows, rows, rows, P(("groups", "ctx")))
    return jax.shard_map(
        on_device, mesh=mesh, in_specs=in_specs, out_specs=(rows,) * 4, check_vma=False
    )
```

```python
import functools

import jax
import jax.numpy as jnp
from jax import lax
from jax.experimental import pallas as pl
from jax.experimental.pallas import tpu as pltpu
from jax.sharding import PartitionSpec as P

HEADS = 8
HEAD_DIM = 64
WIDTH = 512
BLOCK = 128
REACH = 2
LEVELS = 3
BLK_DEV = 2
ROWS = BLK_DEV * BLOCK
PAIR = 2 * HEAD_DIM
PAIRS = WIDTH // PAIR
HALVES = 2
STEPS = PAIRS // HALVES
SPAN = STEPS * PAIR
NEAR = 2 * REACH + 1
SETS = 3 + LEVELS
LEFT = LEVELS
OWN = LEVELS + 1
SCALE = HEAD_DIM ** (-0.5)
MASKED = -1e30


NT = (((1,), (1,)), ((), ()))
NN = (((1,), (0,)), ((), ()))


def dot(a, b, dims):
    return lax.dot_general(a, b, dims, preferred_element_type=jnp.float32)


def two_heads(tile):
    low = lax.broadcasted_iota(jnp.int32, tile.shape, 1) < HEAD_DIM
    zero = jnp.zeros_like(tile)
    return jnp.concatenate([jnp.where(low, tile, zero), jnp.where(low, zero, tile)], axis=0)


def two_heads_turned(tile):
    turned = tile.T
    low = lax.broadcasted_iota(jnp.int32, turned.shape, 0) < HEAD_DIM
    zero = jnp.zeros_like(turned)
    return jnp.concatenate([jnp.where(low, turned, zero), jnp.where(low, zero, turned)], axis=1)


def one_tile(stacked):
    low = lax.broadcasted_iota(jnp.int32, (BLOCK, PAIR), 1) < HEAD_DIM
    return jnp.where(low, stacked[:BLOCK], stacked[BLOCK:])


def attention_kernel(aliased, picks_ref, bias_ref, q_ref, do_ref, *refs):
    key_refs = refs[0 : 2 * SETS : 2]
    value_refs = refs[1 : 2 * SETS : 2]
    out_ref, grad_ref, own_ref, *back_refs = refs[2 * SETS + 2 * aliased :]
    back_refs.insert(OWN, own_ref)

    def gathered(sources, block):
        parts = []
        for offset in range(NEAR):
            source, row = divmod(block + offset, BLK_DEV)
            parts.append(sources[LEFT + source][row * BLOCK : (row + 1) * BLOCK, :])
        for level in range(LEVELS):
            start = pl.multiple_of(picks_ref[block * LEVELS + level] * BLOCK, BLOCK)
            parts.append(sources[level][pl.ds(start, BLOCK), :])
        return jnp.concatenate(parts, axis=0)

    grads = []
    for block in range(BLK_DEV):
        rows = slice(block * BLOCK, (block + 1) * BLOCK)
        tile = (q_ref[rows, :].astype(jnp.float32) * SCALE).astype(jnp.bfloat16)
        cotangent_tile = do_ref[rows, :]
        query = two_heads(tile)
        cotangent = two_heads(cotangent_tile)
        key = gathered(key_refs, block)
        value = gathered(value_refs, block)
        scores = dot(query, key, NT)
        pieces = []
        for j in range(NEAR + LEVELS):
            piece = scores[:, j * BLOCK : (j + 1) * BLOCK]
            if j < NEAR:
                source = (block + j) // BLK_DEV
                if source != 1:
                    piece = piece + bias_ref[source // 2]
            else:
                piece = piece + bias_ref[2 + j - NEAR]
            pieces.append(piece)
        scores = jnp.concatenate(pieces, axis=1)
        peak = jnp.max(scores, axis=1, keepdims=True)
        weights = jnp.exp(scores - peak)
        total = jnp.sum(weights, axis=1, keepdims=True)
        weights = weights * (1.0 / total)
        low = weights.astype(jnp.bfloat16)
        mixed = one_tile(dot(low, value, NN)).astype(jnp.bfloat16)
        out_ref[rows, :] = mixed
        mixed = mixed.astype(jnp.float32)
        delta = jnp.sum(
            cotangent.astype(jnp.float32) * jnp.concatenate([mixed, mixed], axis=0), axis=1, keepdims=True
        )
        grad_weights = dot(cotangent, value, NT)
        grad_scores = (weights * (grad_weights - delta)).astype(jnp.bfloat16)
        grad_query = one_tile(dot(grad_scores, key, NN)) * SCALE
        grad_ref[rows, :] = grad_query.astype(jnp.bfloat16)
        grads.append(
            (
                dot(two_heads_turned(tile), grad_scores, NN),
                dot(two_heads_turned(cotangent_tile), low, NN),
            )
        )
    for which in range(2):
        for source in range(3):
            for row in range(BLK_DEV):
                total = None
                for block in range(BLK_DEV):
                    j = source * BLK_DEV + row - block
                    if 0 <= j < NEAR:
                        term = grads[block][which][:, j * BLOCK : (j + 1) * BLOCK]
                        total = term if total is None else total + term
                back = back_refs[LEFT + source]
                back[which, :, row * BLOCK : (row + 1) * BLOCK] = total.astype(back.dtype)
        for level in range(LEVELS):
            j = NEAR + level
            back = back_refs[level]
            for row in range(BLK_DEV):
                total = None
                for block in range(BLK_DEV):
                    term = grads[block][which][:, j * BLOCK : (j + 1) * BLOCK]
                    term = jnp.where(picks_ref[block * LEVELS + level] == row, term, 0.0)
                    total = term if total is None else total + term
                back[which, :, row * BLOCK : (row + 1) * BLOCK] = total.astype(back.dtype)


def sum_kernel(aliased, own_ref, *refs):
    gk_ref, gv_ref = refs[SETS - 1 + 2 * aliased :]
    for which, out_ref in enumerate((gk_ref, gv_ref)):
        total = own_ref[which]
        for ref in refs[: SETS - 1]:
            total = total + ref[which].astype(jnp.float32)
        out_ref[...] = total.T.astype(out_ref.dtype)


def columns(first):
    return pl.BlockSpec((ROWS, PAIR), lambda p, *_: (0, p + first))


def terms():
    return pl.BlockSpec((2, PAIR, ROWS), lambda p, *_: (0, p, 0))


WHOLE = jax.ShapeDtypeStruct((ROWS, WIDTH), jnp.bfloat16)


def attend(half, picks, bias, queries, grad_out, keys, values, received, earlier):
    first = half * STEPS
    specs = [columns(first), columns(first)]
    operands = [queries, grad_out]
    for index in range(SETS):
        if index == OWN:
            operands += [keys, values]
            specs += [columns(first), columns(first)]
        else:
            source = received[index - (index > OWN)]
            operands += [source, source]
            specs += [columns(0), columns(STEPS)]
    aliases = {}
    if earlier:
        for number, array in enumerate(earlier):
            aliases[len(operands) + 2] = number
            operands.append(array)
            specs.append(pl.BlockSpec(memory_space=pl.ANY))
    own = jax.ShapeDtypeStruct((2, SPAN, ROWS), jnp.float32)
    back = jax.ShapeDtypeStruct((2, SPAN, ROWS), jnp.bfloat16)
    return pl.pallas_call(
        functools.partial(attention_kernel, len(aliases) // 2),
        out_shape=(WHOLE, WHOLE, own, *[back] * (SETS - 1)),
        grid_spec=pltpu.PrefetchScalarGridSpec(
            num_scalar_prefetch=2,
            grid=(STEPS,),
            in_specs=specs,
            out_specs=(columns(first), columns(first), *[terms()] * SETS),
        ),
        input_output_aliases=aliases,
        compiler_params=pltpu.CompilerParams(vmem_limit_bytes=20 * 2**20),
        cost_estimate=pl.CostEstimate(
            flops=4 * 10**9, bytes_accessed=8 * 2**20, transcendentals=2 * 10**6
        ),
        name=f"attention_{half}",
    )(picks, bias, *operands)


def summed(half, own, received, earlier):
    first = half * STEPS
    specs = [terms()] * SETS
    operands = [own, *received]
    aliases = {}
    if earlier:
        for number, array in enumerate(earlier):
            aliases[len(operands)] = number
            operands.append(array)
            specs.append(pl.BlockSpec(memory_space=pl.ANY))
    return pl.pallas_call(
        functools.partial(sum_kernel, len(aliases) // 2),
        out_shape=(WHOLE, WHOLE),
        grid=(STEPS,),
        in_specs=specs,
        out_specs=(columns(first), columns(first)),
        input_output_aliases=aliases,
        compiler_params=pltpu.CompilerParams(vmem_limit_bytes=8 * 2**20),
        cost_estimate=pl.CostEstimate(
            flops=10**6, bytes_accessed=4 * 2**20, transcendentals=0
        ),
        name=f"grad_sum_{half}",
    )(*operands)


def on_device(queries, keys, values, grad_out, far_blocks, far_levels):
    size = lax.axis_size("ctx")
    index = lax.axis_index("ctx")
    top_bit = size.bit_length() - 2

    def exchanged(array, level):
        return lax.ppermute(array, "ctx", [(i, i ^ 1 << (top_bit - level)) for i in range(size)])

    def moved(array, by):
        pairs = [(i, i + by) for i in range(size) if 0 <= i + by < size]
        return lax.ppermute(array, "ctx", pairs)

    received = []
    for half in range(HALVES):
        part = slice(half * SPAN, (half + 1) * SPAN)
        key_value = jnp.concatenate([keys[:, part], values[:, part]], axis=1)
        far = [exchanged(key_value, level) for level in range(LEVELS)]
        received.append(far + [moved(key_value, 1), moved(key_value, -1)])

    picks = (far_blocks % BLK_DEV).reshape(-1)
    used = jnp.arange(LEVELS, dtype=jnp.int32) < far_levels[0]
    edges = jnp.stack([index > 0, index < size - 1])
    bias = jnp.where(jnp.concatenate([edges, used]), 0.0, MASKED).astype(jnp.float32)

    outs = None
    owns = []
    returned = []
    for half in range(HALVES):
        *outs, own, back0, back1, back2, left, right = attend(
            half, picks, bias, queries, grad_out, keys, values, received[half], outs
        )
        owns.append(own)
        far = [exchanged(back, level) for level, back in enumerate((back0, back1, back2))]
        returned.append(far + [moved(left, -1), moved(right, 1)])
    grads = None
    for half in range(HALVES):
        grads = summed(half, owns[half], returned[half], grads)
    return (*outs, *grads)


def solution(mesh):
    rows = P(("groups", "ctx"), None)
    in_specs = (rows, rows, rows, rows, rows, P(("groups", "ctx")))
    return jax.shard_map(
        on_device, mesh=mesh, in_specs=in_specs, out_specs=(rows,) * 4, check_vma=False
    )
```

```python
import functools

import jax
import jax.numpy as jnp
from jax import lax
from jax.experimental import pallas as pl
from jax.experimental.pallas import tpu as pltpu
from jax.sharding import PartitionSpec as P


HEAD_DIM = 64
WIDTH = 512
BLOCK = 128
REACH = 2
LEVELS = 3
BLK_DEV = 2
ROWS = BLK_DEV * BLOCK
PAIR = 2 * HEAD_DIM
PAIRS = WIDTH // PAIR
HALVES = 2
STEPS = PAIRS // HALVES
SPAN = STEPS * PAIR
NEAR = 2 * REACH + 1
SETS = 3 + LEVELS
KEY_ORDER = ((1, 0, 2, "right", "left"), (2, "right", "left", 0, 1))
GRAD_ORDER = (1, 0, 2, "right", "left")
SCALE = HEAD_DIM ** (-0.5)
MASKED = -1e30


NT = (((1,), (1,)), ((), ()))
NN = (((1,), (0,)), ((), ()))


def dot(a, b, dims):
    return lax.dot_general(a, b, dims, preferred_element_type=jnp.float32)


def two_heads(tile):
    low = lax.broadcasted_iota(jnp.int32, tile.shape, 1) < HEAD_DIM
    zero = jnp.zeros_like(tile)
    return jnp.concatenate([jnp.where(low, tile, zero), jnp.where(low, zero, tile)], axis=0)


def two_heads_turned(tile):
    turned = tile.T
    low = lax.broadcasted_iota(jnp.int32, turned.shape, 0) < HEAD_DIM
    zero = jnp.zeros_like(turned)
    return jnp.concatenate([jnp.where(low, turned, zero), jnp.where(low, zero, turned)], axis=1)


def one_tile(stacked):
    low = lax.broadcasted_iota(jnp.int32, (BLOCK, PAIR), 1) < HEAD_DIM
    return jnp.where(low, stacked[:BLOCK], stacked[BLOCK:])


def attention_kernel(half, picks_ref, bias_ref, q_ref, do_ref, *refs):
    names = ("own",) + KEY_ORDER[half]
    keys = dict(zip(names, refs[0 : 2 * SETS : 2]))
    values = dict(zip(names, refs[1 : 2 * SETS : 2]))
    at = 2 * SETS + (2 if half else 0)
    out_ref, grad_ref, own_ref = refs[at : at + 3]
    backs = dict(zip(GRAD_ORDER, refs[at + 3 :]), own=own_ref)
    sides = ("left", "own", "right")

    def gathered(source, block):
        parts = []
        for offset in range(NEAR):
            side, row = divmod(block + offset, BLK_DEV)
            rows = slice(row * BLOCK, (row + 1) * BLOCK)
            parts.append(source[sides[side]][rows, :])
        for level in range(LEVELS):
            start = pl.multiple_of(picks_ref[block * LEVELS + level] * BLOCK, BLOCK)
            parts.append(source[level][pl.ds(start, BLOCK), :])
        return jnp.concatenate(parts, axis=0)

    grads = []
    for block in range(BLK_DEV):
        rows = slice(block * BLOCK, (block + 1) * BLOCK)
        tile = (q_ref[rows, :].astype(jnp.float32) * SCALE).astype(jnp.bfloat16)
        cotangent_tile = do_ref[rows, :]
        query = two_heads(tile)
        cotangent = two_heads(cotangent_tile)
        key = gathered(keys, block)
        value = gathered(values, block)
        scores = dot(query, key, NT)
        pieces = []
        for j in range(NEAR + LEVELS):
            piece = scores[:, j * BLOCK : (j + 1) * BLOCK]
            if j < NEAR:
                source = (block + j) // BLK_DEV
                if source != 1:
                    piece = piece + bias_ref[source // 2]
            else:
                piece = piece + bias_ref[2 + j - NEAR]
            pieces.append(piece)
        scores = jnp.concatenate(pieces, axis=1)
        peak = jnp.max(scores, axis=1, keepdims=True)
        weights = jnp.exp(scores - peak)
        total = jnp.sum(weights, axis=1, keepdims=True)
        weights = weights * (1.0 / total)
        low = weights.astype(jnp.bfloat16)
        mixed = one_tile(dot(low, value, NN)).astype(jnp.bfloat16)
        out_ref[rows, :] = mixed
        mixed = mixed.astype(jnp.float32)
        delta = jnp.sum(
            cotangent.astype(jnp.float32) * jnp.concatenate([mixed, mixed], axis=0), axis=1, keepdims=True
        )
        grad_weights = dot(cotangent, value, NT)
        grad_scores = (weights * (grad_weights - delta)).astype(jnp.bfloat16)
        grad_query = one_tile(dot(grad_scores, key, NN)) * SCALE
        grad_ref[rows, :] = grad_query.astype(jnp.bfloat16)
        grads.append(
            (
                dot(two_heads_turned(tile), grad_scores, NN),
                dot(two_heads_turned(cotangent_tile), low, NN),
            )
        )
    for which in range(2):
        for source, side in enumerate(sides):
            back = backs[side]
            for row in range(BLK_DEV):
                total = None
                for block in range(BLK_DEV):
                    j = source * BLK_DEV + row - block
                    if 0 <= j < NEAR:
                        term = grads[block][which][:, j * BLOCK : (j + 1) * BLOCK]
                        total = term if total is None else total + term
                back[which, :, row * BLOCK : (row + 1) * BLOCK] = total.astype(back.dtype)
        for level in range(LEVELS):
            j = NEAR + level
            back = backs[level]
            for row in range(BLK_DEV):
                total = None
                for block in range(BLK_DEV):
                    term = grads[block][which][:, j * BLOCK : (j + 1) * BLOCK]
                    term = jnp.where(picks_ref[block * LEVELS + level] == row, term, 0.0)
                    total = term if total is None else total + term
                back[which, :, row * BLOCK : (row + 1) * BLOCK] = total.astype(back.dtype)


def sum_kernel(count, *refs):
    for which, out_ref in enumerate(refs[-2:]):
        total = refs[0][which]
        for ref in refs[1:count]:
            total = total + ref[which].astype(jnp.float32)
        out_ref[...] = total.T.astype(out_ref.dtype)


def columns(first):
    return pl.BlockSpec((ROWS, PAIR), lambda p, *_: (0, p + first))


def terms():
    return pl.BlockSpec((2, PAIR, ROWS), lambda p, *_: (0, p, 0))


WHOLE = jax.ShapeDtypeStruct((ROWS, WIDTH), jnp.bfloat16)


def attend(half, picks, bias, queries, grad_out, keys, values, received, earlier):
    first = half * STEPS
    specs = [columns(first)] * 4
    operands = [queries, grad_out, keys, values]
    for name in KEY_ORDER[half]:
        source = received[name]
        operands += [source, source]
        specs += [columns(0), columns(STEPS)]
    aliases = {}
    if earlier:
        for number, array in enumerate(earlier):
            aliases[len(operands) + 2] = number
            operands.append(array)
            specs.append(pl.BlockSpec(memory_space=pl.ANY))
    own = jax.ShapeDtypeStruct((2, SPAN, ROWS), jnp.float32)
    back = jax.ShapeDtypeStruct((2, SPAN, ROWS), jnp.bfloat16)
    return pl.pallas_call(
        functools.partial(attention_kernel, half),
        out_shape=(WHOLE, WHOLE, own, *[back] * (SETS - 1)),
        grid_spec=pltpu.PrefetchScalarGridSpec(
            num_scalar_prefetch=2,
            grid=(STEPS,),
            in_specs=specs,
            out_specs=(columns(first), columns(first), *[terms()] * SETS),
        ),
        input_output_aliases=aliases,
        compiler_params=pltpu.CompilerParams(vmem_limit_bytes=20 * 2**20),
        cost_estimate=pl.CostEstimate(
            flops=4 * 10**9, bytes_accessed=8 * 2**20, transcendentals=2 * 10**6
        ),
    )(picks, bias, *operands)


def summed(half, own, received, earlier):
    first = half * STEPS
    operands = [own, *received]
    count = len(operands)
    specs = [terms()] * count
    aliases = {}
    if earlier:
        for number, array in enumerate(earlier):
            aliases[len(operands)] = number
            operands.append(array)
            specs.append(pl.BlockSpec(memory_space=pl.ANY))
    return pl.pallas_call(
        functools.partial(sum_kernel, count),
        out_shape=(WHOLE, WHOLE),
        grid=(STEPS,),
        in_specs=specs,
        out_specs=(columns(first), columns(first)),
        input_output_aliases=aliases,
        compiler_params=pltpu.CompilerParams(vmem_limit_bytes=8 * 2**20),
        cost_estimate=pl.CostEstimate(
            flops=10**6, bytes_accessed=4 * 2**20, transcendentals=0
        ),
    )(*operands)


def step(queries, keys, values, grad_out, far_blocks, far_levels):
    size = lax.axis_size("ctx")
    index = lax.axis_index("ctx")
    top_bit = size.bit_length() - 2

    def sent(array, pairs):
        return lax.ppermute(array, "ctx", pairs)

    def exchanged(array, level):
        return sent(array, [(i, i ^ 1 << (top_bit - level)) for i in range(size)])

    def moved(array, by):
        pairs = [(i, i + by) for i in range(size) if 0 <= i + by < size]
        return sent(array, pairs)

    received = []
    for half in range(HALVES):
        part = slice(half * SPAN, (half + 1) * SPAN)
        key_value = jnp.concatenate([keys[:, part], values[:, part]], axis=1)
        arrays = {level: exchanged(key_value, level) for level in range(LEVELS)}
        arrays["left"] = moved(key_value, 1)
        arrays["right"] = moved(key_value, -1)
        received.append(arrays)

    picks = (far_blocks % BLK_DEV).reshape(-1)
    used = jnp.arange(LEVELS, dtype=jnp.int32) < far_levels[0]
    edges = jnp.stack([index > 0, index < size - 1])
    bias = jnp.where(jnp.concatenate([edges, used]), 0.0, MASKED).astype(jnp.float32)

    outs = None
    owns = []
    returned = []
    for half in range(HALVES):
        outs = attend(
            half, picks, bias, queries, grad_out, keys, values, received[half], outs
        )
        outs, own, backs = outs[:2], outs[2], outs[3:]
        owns.append(own)
        terms_in = []
        for name, back in zip(GRAD_ORDER, backs):
            if name == "left":
                terms_in.append(moved(back, -1))
            elif name == "right":
                terms_in.append(moved(back, 1))
            else:
                terms_in.append(exchanged(back, name))
        returned.append(terms_in)
    grads = None
    for half in range(HALVES):
        grads = summed(half, owns[half], returned[half], grads)
    return (*outs, *grads)


def solution(mesh):
    rows = P(("groups", "ctx"), None)
    in_specs = (rows, rows, rows, rows, rows, P(("groups", "ctx")))
    return jax.shard_map(step, mesh=mesh, in_specs=in_specs, out_specs=(rows,) * 4, check_vma=False)
```
